256 devices in a mesh: sky: 64 (over z, x, core), grp: 4 (over y).
Axes of the slice: x: 4, y: 4, z: 8, core: 2. Of those that a mesh axis runs over, the one named last changes fastest.
Arguments:
- sky_strip: float32 [64, 32768], P(None, 'sky'), may hold values from -6 to 6
- exposures: float32 [1024, 64, 2048], P(('sky', 'grp')), may hold values from -6 to 6
- psf_taps: float32 [1024, 256], P(('sky', 'grp')), may hold values from -0.375 to 0.375
- offsets: int32 [1024], P(('sky', 'grp')), may hold values from 0 to 511
- counts: int32 [256], P(('sky', 'grp')), may hold values from 1 to 4, as said below
- features: bfloat16 [128, 64, 32768], P(None, None, 'sky'), may hold values from -6 to 6
- conv_weight: bfloat16 [128, 3, 3, 128], P('grp'), may hold values from -0.1875 to 0.1875
- conv_bias: float32 [128], P('grp'), may hold values from -4 to 4
- out_weight: float32 [128], P('grp'), may hold values from -0.5 to 0.5
Outputs:
- score_map: float32 [64, 32768], P('grp', 'sky')
The draws below stay inside these ranges and needn't reach their ends.
Inputs may be any that keep to these rules, and one draw needn't show every extreme that they name: Slots 0 to counts[d] - 1 of device d hold exposures; some device uses all 4 slots and some only one.
All inputs are finite; a program needn't handle non-finite values.
Results may differ from the reference program's by a relative error of at most 0.0003.
Values may be sent and summed in bfloat16 or wider, within the bound.
No kernel may reach another device: no remote copies, remote signals or barrier semaphores. Data moves between devices by JAX's collectives and lax.ppermute only.
A program may use at most 128 MiB of HBM per device.

```python
import jax
import jax.numpy as jnp
from jax import lax

TILE = 256
TILES_DEV = 2
EW = 2048
PSF_W = 256
CH = 128
TR = 64
E_DEV = 4
CW = 512
NCOL = 32768
EXPO = 1024
N_SKY = 64
N_GRP = 4


def draw_counts(key, part):
    total = EXPO // E_DEV
    values = jax.random.randint(key, (total,), 1, E_DEV + 1, dtype=jnp.int32)
    chosen = jax.random.randint(jax.random.fold_in(key, 7), (), 0, total, dtype=jnp.int32)
    lowest = (chosen + total // 2) % total
    values = values.at[chosen].set(E_DEV)
    return values.at[lowest].set(1)


def place_ends(array, key, smallest, top_value):
    place = [jax.random.randint(jax.random.fold_in(key, axis), (), 0, length) for axis, length in enumerate(array.shape)]
    longest = array.shape.index(max(array.shape))
    beside = place[:longest] + [(place[longest] + 1) % array.shape[longest]] + place[longest + 1:]
    return array.at[tuple(place)].set(smallest).at[tuple(beside)].set(top_value)


def shard_levels(rng, shape, shards, smallest, largest):
    factor_of = 1.0
    for dim, blocks in shards:
        draws = jax.random.uniform(jax.random.fold_in(jax.random.fold_in(rng, 6), dim), (blocks,), jnp.float32, smallest / len(shards), largest / len(shards))
        factor_of = factor_of * jnp.repeat(jnp.exp(draws), shape[dim] // blocks).reshape((-1,) + (1,) * (len(shape) - 1 - dim))
    return factor_of


def bell_draw(key, shape, scale, limit, shards=(), kind=jnp.bfloat16):
    entries = jax.random.normal(key, shape, jnp.float32) * scale
    if len(shards) > 0:
        entries = shard_levels(key, shape, shards, -0.22, 0.18) * entries
    return jnp.clip(entries, min=-limit, max=limit).astype(kind)


def setup_inputs(seed: int = 0) -> dict:
    keys = jax.random.split(jax.random.key(seed), 10)
    return {
        "sky_strip": bell_draw(keys[0], (TR, NCOL), 1.0, 6.0, ((1, 64),), jnp.float32),
        "exposures": bell_draw(keys[1], (EXPO, TR, EW), 1.0, 6.0, ((0, 256),), jnp.float32),
        "psf_taps": bell_draw(keys[2], (EXPO, PSF_W), PSF_W ** -0.5, 0.375, ((0, 256),), jnp.float32),
        "offsets": place_ends(jax.random.randint(keys[3], (EXPO,), 0, CW), jax.random.fold_in(keys[3], 1), 0, CW - 1).astype(jnp.int32),
        "counts": draw_counts(jax.random.fold_in(keys[9], 71), 0),
        "features": bell_draw(keys[5], (CH, TR, NCOL), 1.0, 6.0, ((2, 64),)),
        "conv_weight": bell_draw(keys[6], (CH, 3, 3, CH), (9 * CH) ** -0.5, 0.1875, ((0, 4),)),
        "conv_bias": bell_draw(keys[7], (CH,), 1.0, 4.0, ((0, 4),), jnp.float32),
        "out_weight": bell_draw(keys[8], (CH,), CH ** -0.5, 0.5, ((0, 4),), jnp.float32),
    }


def reference(sky_strip, exposures, psf_taps, offsets, counts, features, conv_weight, conv_bias, out_weight):
    total_cols = sky_strip.shape[1]
    block_cols = TILE * TILES_DEV
    per_block = N_GRP * E_DEV
    kernel_spectrum = jnp.fft.rfft(jnp.pad(psf_taps, ((0, 0), (0, EW - PSF_W))), axis=-1)
    lane_offsets = jnp.arange(EW, dtype=jnp.int32)

    def visit(adjoint, scan_item):
        expo_index, record, spectrum, offset = scan_item
        first_column = (expo_index // per_block) * block_cols + offset
        columns = (first_column + lane_offsets) % total_cols
        window = jnp.take(sky_strip, columns, axis=1)
        model = jnp.fft.irfft(jnp.fft.rfft(window, axis=-1) * spectrum, n=EW, axis=-1)
        live_flag = ((expo_index % E_DEV) < counts[expo_index // E_DEV]).astype(sky_strip.dtype)
        residual = (record - model) * live_flag
        adjoint_rows = jnp.fft.irfft(jnp.fft.rfft(residual, axis=-1) * jnp.conj(spectrum), n=EW, axis=-1)
        return adjoint.at[:, columns].add(adjoint_rows.astype(adjoint.dtype)), None

    adjoint, _ = lax.scan(visit, jnp.zeros_like(sky_strip),
                          (jnp.arange(EXPO, dtype=jnp.int32), exposures, kernel_spectrum, offsets))

    wrapped = jnp.concatenate([features[:, :, -1:], features, features[:, :, :1]], axis=2)
    kernel_oihw = jnp.transpose(conv_weight, (0, 3, 1, 2)).astype(jnp.float32)

    def denoise(block_index):
        piece = lax.dynamic_slice_in_dim(wrapped, block_index * block_cols, block_cols + 2, axis=2).astype(jnp.float32)
        hidden = lax.conv_general_dilated(piece[None], kernel_oihw, (1, 1), ((1, 1), (0, 0)),
                                          dimension_numbers=("NCHW", "OIHW", "NCHW"),
                                          precision=lax.Precision.HIGHEST)[0]
        hidden = hidden + conv_bias[:, None, None]
        return jnp.sum(out_weight[:, None, None] * jax.nn.silu(hidden), axis=0)

    prior = lax.map(denoise, jnp.arange(N_SKY, dtype=jnp.int32))
    prior = jnp.transpose(prior, (1, 0, 2)).reshape(TR, total_cols)
    return adjoint + prior
```

```python
import functools

import jax
import jax.numpy as jnp
from jax import lax
from jax.experimental import pallas as pl
from jax.experimental.pallas import tpu as pltpu
from jax.sharding import PartitionSpec as P

F32 = jnp.float32
BF16 = jnp.bfloat16
LANES = 128


def shifted(x, axis, by):
    length = lax.axis_size(axis)
    return lax.ppermute(x, axis, [(i, (i + by) % length) for i in range(length)])


def partner(x, axis, mask):
    return lax.ppermute(x, axis, [(i, i ^ mask) for i in range(lax.axis_size(axis))])


def lane_index(shape):
    return lax.broadcasted_iota(jnp.int32, shape, 1)


def column(row):
    n = row.shape[1]
    spread = jnp.broadcast_to(row, (n, n))
    diagonal = lax.broadcasted_iota(jnp.int32, (n, n), 0) == lane_index((n, n))
    return jnp.sum(jnp.where(diagonal, spread, 0.0), axis=1, keepdims=True)


def weighted_silu(hidden, half_weight):
    return hidden * (1.0 + jnp.tanh(0.5 * hidden)) * half_weight


def conv_kernel(w_ref, bias_ref, ow_ref, x_ref, prior_ref, left_ref, right_ref, t_ref, p_ref, carry_ref):
    step = pl.program_id(0)
    channels, rows, cols = x_ref.shape
    outs = bias_ref.shape[1]
    taps = 3 * outs
    depth = channels * rows

    @pl.when(step == 0)
    def _():
        repeat = jnp.where(
            lane_index((channels, depth)) // rows == lax.broadcasted_iota(jnp.int32, (channels, depth), 0), 1.0, 0.0
        ).astype(BF16)
        spread = jnp.dot(w_ref[...], repeat, preferred_element_type=F32)
        row_in = lane_index((taps, depth)) % rows
        for j in range(rows + 2):
            band = jnp.zeros((taps, depth), F32)
            for a in range(3):
                band = jnp.where(row_in == j - 2 + a, spread[a * taps : (a + 1) * taps], band)
            t_ref[j * taps : (j + 1) * taps, :] = band.astype(BF16)
        carry_ref[...] = jnp.zeros_like(carry_ref)
        left_ref[...] = jnp.zeros_like(left_ref)
        right_ref[...] = jnp.zeros_like(right_ref)

    @pl.when(step > 0)
    def _():
        carry_ref[...] = p_ref[rows * taps :, :]

    x = x_ref[...].reshape(depth, cols)
    p_ref[...] = jnp.dot(t_ref[...], x, preferred_element_type=F32)

    bias = column(bias_ref[...])
    half_weight = column(ow_ref[...]) * 0.5
    lane = lane_index((1, LANES))
    col = lane_index((1, cols))
    inner = jnp.logical_and(col > 0, col < cols - 1)

    def one_row(i, carried):
        row = step * rows - 1 + i
        parts = []
        for b in range(3):
            part = p_ref[i * taps + b * outs : i * taps + (b + 1) * outs, :]
            if carried:
                part = part + carry_ref[i * taps + b * outs : i * taps + (b + 1) * outs, :]
            parts.append(part)
        before, here, after = parts
        hidden = pltpu.roll(before, 1, 1) + here + pltpu.roll(after, cols - 1, 1) + bias
        score = jnp.sum(weighted_silu(hidden, half_weight), axis=0, keepdims=True)
        prior_ref[pl.ds(row, 1), :] = jnp.where(inner, score, 0.0)
        mine = (lane >> 1) == row
        tail = before[:, cols - LANES :] + jnp.where(
            lane == LANES - 2, pltpu.roll(here[:, cols - LANES :], LANES - 1, 1), 0.0
        )
        left_ref[...] += jnp.where(mine, pltpu.roll(tail, 2 * row + 2, 1), 0.0)
        head = after[:, :LANES] + jnp.where(lane == 1, pltpu.roll(here[:, :LANES], 1, 1), 0.0)
        right_ref[...] += jnp.where(mine, pltpu.roll(head, 2 * row, 1), 0.0)

    @pl.when(step > 0)
    def _():
        one_row(0, True)

    for i in range(1, rows):
        one_row(i, i < 2)

    @pl.when(step == pl.num_programs(0) - 1)
    def _():
        one_row(rows, False)


def conv_prior(features, weight, bias, out_weight):
    channels, strip_rows, cols = features.shape
    outs = bias.shape[0]
    rows = 8
    taps = 3 * outs
    flat = weight.transpose(1, 2, 0, 3).reshape(9 * outs, channels)
    full = lambda shape: pl.BlockSpec(shape, lambda i: (0,) * len(shape))
    return pl.pallas_call(
        conv_kernel,
        grid=(strip_rows // rows,),
        in_specs=[
            full((9 * outs, channels)),
            full((1, outs)),
            full((1, outs)),
            pl.BlockSpec((channels, rows, cols), lambda i: (0, i, 0)),
        ],
        out_specs=[full((strip_rows, cols)), full((outs, LANES)), full((outs, LANES))],
        out_shape=[
            jax.ShapeDtypeStruct((strip_rows, cols), F32),
            jax.ShapeDtypeStruct((outs, LANES), F32),
            jax.ShapeDtypeStruct((outs, LANES), F32),
        ],
        scratch_shapes=[
            pltpu.VMEM(((rows + 2) * taps, channels * rows), BF16),
            pltpu.VMEM(((rows + 2) * taps, cols), F32),
            pltpu.VMEM((2 * taps, cols), F32),
        ],
        compiler_params=pltpu.CompilerParams(vmem_limit_bytes=40 << 20),
        cost_estimate=pl.CostEstimate(flops=8_000_000_000, bytes_accessed=9_000_000, transcendentals=1_000_000),
    )(flat, bias.reshape(1, outs), out_weight.reshape(1, outs), features)


def split(x):
    high = x.astype(BF16)
    return high, (x - high.astype(F32)).astype(BF16)


def exposure_kernel(
    offsets_ref, counts_ref, group_ref, s0, s1, s2, s3, s4, record_ref, taps_ref, prior_ref, left_ref, right_ref,
    bias_ref, ow_ref, o0, o1, o2, o3, ext_ref, acc_ref,
):
    slot = pl.program_id(0)
    rows, cols = s0.shape
    width = record_ref.shape[2]
    tap_count = taps_ref.shape[2]
    pieces = width // tap_count
    tiles = width // LANES

    @pl.when(slot == 0)
    def _():
        for d, part in enumerate((s0, s1, s2, s3, s4)):
            ext_ref[:, d * cols : (d + 1) * cols] = part[...]
        acc_ref[:, cols:] = jnp.zeros((rows, acc_ref.shape[1] - cols), F32)
        acc_ref[:, :cols] = prior_ref[...]
        edge = left_ref[...] + right_ref[...] + column(bias_ref[...])
        score = jnp.sum(weighted_silu(edge, column(ow_ref[...]) * 0.5), axis=0, keepdims=True)
        lane = lane_index((rows, LANES))
        own = jnp.where((lane >> 1) == lax.broadcasted_iota(jnp.int32, (rows, LANES), 0), score, 0.0)
        last = jnp.sum(jnp.where((lane & 1) == 0, own, 0.0), axis=1, keepdims=True)
        following = jnp.sum(jnp.where((lane & 1) == 1, own, 0.0), axis=1, keepdims=True)
        acc_ref[:, cols - LANES : cols] += jnp.where(lane == LANES - 1, last, 0.0)
        acc_ref[:, cols : cols + LANES] += jnp.where(lane == 0, following, 0.0)

    @pl.when(slot < counts_ref[0])
    def _():
        offset = offsets_ref[slot]
        rest = offset % LANES
        base = pl.multiple_of(offset - rest, LANES)
        lane = lane_index((rows, LANES))

        taps = taps_ref[0]
        wide = jnp.concatenate([taps, jnp.zeros_like(taps)], axis=1)
        band = pltpu.roll(jnp.broadcast_to(wide, (tap_count, 2 * tap_count)), 0, 1, stride=1, stride_axis=0)
        band_high, band_low = split(band)

        turned = [
            pltpu.roll(ext_ref[:, pl.ds(base + m * LANES, LANES)], LANES - rest, 1) for m in range(tiles + 1)
        ]
        keep = lane < LANES - rest
        window = [jnp.where(keep, turned[m], turned[m + 1]) for m in range(tiles)]
        per = tap_count // LANES

        def stacked(parts):
            return jnp.concatenate(
                [jnp.concatenate(parts[n * per : (n + 1) * per], axis=1) for n in range(pieces)], axis=0
            )

        def product(x, matrix, dims):
            return lax.dot_general(x, matrix, (dims, ((), ())), preferred_element_type=F32)

        def banded(x, shift, dims):
            high, low = split(x)
            total = None
            for at, columns in ((0, 0), (shift, 1)):
                cut = slice(columns * tap_count, (columns + 1) * tap_count)
                x_high, x_low = high, low
                if at:
                    k = (at * rows) % x.shape[0]
                    x_high = jnp.concatenate([high[k:], high[:k]], axis=0)
                    x_low = jnp.concatenate([low[k:], low[:k]], axis=0)
                part = (
                    product(x_high, band_high[:, cut], dims)
                    + product(x_low, band_high[:, cut], dims)
                    + product(x_high, band_low[:, cut], dims)
                )
                total = part if total is None else total + part
            return total

        model = banded(stacked(window), pieces - 1, ((1,), (0,)))
        record = record_ref[0]
        residual = (
            jnp.concatenate([record[:, n * tap_count : (n + 1) * tap_count] for n in range(pieces)], axis=0) - model
        )
        back = banded(residual, 1, ((1,), (1,)))
        moved = []
        for m in range(tiles):
            n, h = divmod(m, per)
            moved.append(pltpu.roll(back[n * rows : (n + 1) * rows, h * LANES : (h + 1) * LANES], rest, 1))
        nothing = jnp.zeros((rows, LANES), F32)
        spill = lane < rest
        for m in range(tiles + 1):
            inside = moved[m] if m < tiles else nothing
            earlier = moved[m - 1] if m > 0 else nothing
            acc_ref[:, pl.ds(base + m * LANES, LANES)] += jnp.where(spill, earlier, inside)

    @pl.when(slot == pl.num_programs(0) - 1)
    def _():
        share = o0.shape[0]
        for k, out in enumerate((o0, o1, o2, o3)):
            first = pl.multiple_of((group_ref[0] ^ k) * share, share)
            out[...] = acc_ref[pl.ds(first, share), :]


def exposure_terms(group, offsets, counts, sky_parts, exposures, psf_taps, prior, left, right, bias, out_weight, n_grp):
    slots, rows, width = exposures.shape
    cols = sky_parts[0].shape[1]
    reach = len(sky_parts) * cols
    outs = bias.shape[0]
    share = rows // n_grp
    full = lambda shape: pl.BlockSpec(shape, lambda i, *_: (0,) * len(shape))
    return pl.pallas_call(
        exposure_kernel,
        grid_spec=pltpu.PrefetchScalarGridSpec(
            num_scalar_prefetch=3,
            grid=(slots,),
            in_specs=[full((rows, cols))] * len(sky_parts)
            + [
                pl.BlockSpec((1, rows, width), lambda i, *_: (i, 0, 0)),
                pl.BlockSpec((1, 1, psf_taps.shape[1]), lambda i, *_: (i, 0, 0)),
                full((rows, cols)),
                full((outs, LANES)),
                full((outs, LANES)),
                full((1, outs)),
                full((1, outs)),
            ],
            out_specs=[full((share, reach))] * n_grp,
            scratch_shapes=[pltpu.VMEM((rows, reach), F32), pltpu.VMEM((rows, reach), F32)],
        ),
        out_shape=[jax.ShapeDtypeStruct((share, reach), F32)] * n_grp,
        compiler_params=pltpu.CompilerParams(vmem_limit_bytes=40 << 20),
        cost_estimate=pl.CostEstimate(flops=4_000_000_000, bytes_accessed=4_000_000, transcendentals=0),
    )(
        offsets, counts, group, *sky_parts, exposures, psf_taps.reshape(slots, 1, -1), prior, left, right,
        bias.reshape(1, outs), out_weight.reshape(1, outs),
    )


def sum_kernel(a, b, c, d, *outs):
    total = a[...] + b[...] + c[...] + d[...]
    cols = outs[0].shape[1]
    for k, out in enumerate(outs):
        out[...] = total[:, k * cols : (k + 1) * cols]


def on_device(
    sky_strip, exposures, psf_taps, offsets, counts, features, conv_weight, conv_bias, out_weight
):
    n_grp = lax.axis_size("grp")
    cols = sky_strip.shape[1]
    reach_blocks = exposures.shape[2] // cols
    parts = [sky_strip]
    for distance in range(1, reach_blocks + 1):
        parts.append(shifted(sky_strip, "sky", -distance))
    prior, left, right = conv_prior(features, conv_weight, conv_bias, out_weight)
    right = shifted(right, "sky", -1)
    group = lax.axis_index("grp").astype(jnp.int32).reshape(1)
    terms = exposure_terms(
        group, offsets, counts, parts, exposures, psf_taps, prior, left, right, conv_bias, out_weight, n_grp
    )
    received = [terms[0]] + [partner(terms[k], "grp", k) for k in range(1, n_grp)]
    share = terms[0].shape[0]
    pieces = pl.pallas_call(
        sum_kernel,
        out_shape=[jax.ShapeDtypeStruct((share, cols), F32)] * (reach_blocks + 1),
        cost_estimate=pl.CostEstimate(flops=200_000, bytes_accessed=1_000_000, transcendentals=0),
    )(*received)
    total = pieces[0]
    for distance in range(1, reach_blocks + 1):
        total = total + shifted(pieces[distance], "sky", distance)
    return total


def solution(mesh):
    placed = (
        P(None, "sky"),
        P(("sky", "grp"), None, None),
        P(("sky", "grp"), None),
        P(("sky", "grp")),
        P(("sky", "grp")),
        P(None, None, "sky"),
        P("grp", None, None, None),
        P("grp"),
        P("grp"),
    )
    return jax.shard_map(
        on_device, mesh=mesh, in_specs=placed, out_specs=P("grp", "sky"), check_vma=False
    )
```

```python
import functools

import jax
import jax.numpy as jnp
from jax import lax
from jax.experimental import pallas as pl
from jax.experimental.pallas import tpu as pltpu
from jax.sharding import PartitionSpec as P

F32 = jnp.float32
BF16 = jnp.bfloat16
LANES = 128


def shifted(x, axis, by):
    length = lax.axis_size(axis)
    return lax.ppermute(x, axis, [(i, (i + by) % length) for i in range(length)])


def partner(x, axis, mask):
    return lax.ppermute(x, axis, [(i, i ^ mask) for i in range(lax.axis_size(axis))])


def lane_index(shape):
    return lax.broadcasted_iota(jnp.int32, shape, 1)


def column(row):
    n = row.shape[1]
    spread = jnp.broadcast_to(row, (n, n))
    diagonal = lax.broadcasted_iota(jnp.int32, (n, n), 0) == lane_index((n, n))
    return jnp.sum(jnp.where(diagonal, spread, 0.0), axis=1, keepdims=True)


def weighted_silu(hidden, half_weight):
    return hidden * (1.0 + jnp.tanh(0.5 * hidden)) * half_weight


def conv_kernel(w_ref, bias_ref, ow_ref, *refs):
    x_refs, (prior_ref, left_ref, right_ref, t_ref, a_ref, b_ref) = refs[:-6], refs[-6:]
    step = pl.program_id(0)
    channels = w_ref.shape[1]
    cols = prior_ref.shape[1]
    outs = bias_ref.shape[1]
    taps = 3 * outs
    block = 8
    pairs = block // 2

    @pl.when(step == 0)
    def _():
        w = [w_ref[a * taps : (a + 1) * taps, :] for a in range(3)]
        none = jnp.zeros_like(w[0])
        for j, (even, odd) in enumerate(((w[2], none), (w[1], w[2]), (w[0], w[1]), (none, w[0]))):
            t_ref[j * taps : (j + 1) * taps, :channels] = even
            t_ref[j * taps : (j + 1) * taps, channels:] = odd
        b_ref[pairs - 1] = jnp.zeros(b_ref.shape[1:], F32)
        left_ref[...] = jnp.zeros_like(left_ref)
        right_ref[...] = jnp.zeros_like(right_ref)

    bias = column(bias_ref[...])
    half_weight = column(ow_ref[...]) * 0.5
    lane = lane_index((outs, LANES))
    col = lane_index((1, cols))
    inner = jnp.logical_and(col > 0, col < cols - 1)

    def load(half):
        parts = [jnp.swapaxes(x[:, half * block : (half + 1) * block, :], 0, 1) for x in x_refs]
        return jnp.concatenate(parts, axis=1)

    def multiply(p_ref, x, pair):
        both = x[2 * pair : 2 * pair + 2].reshape(2 * channels, cols)
        p_ref[pair] = jnp.dot(t_ref[...], both, preferred_element_type=F32)

    def finish(first, terms, base, r, edges):
        (p1, n1, j1), (p2, n2, j2) = terms
        before, here, after = [
            p1[n1, j1 * taps + b * outs : j1 * taps + (b + 1) * outs, :]
            + p2[n2, j2 * taps + b * outs : j2 * taps + (b + 1) * outs, :]
            for b in range(3)
        ]
        last_row(before, here, after, base, r, edges)

    def last_row(before, here, after, base, r, edges):
        hidden = pltpu.roll(before, 1, 1) + here + pltpu.roll(after, cols - 1, 1) + bias
        score = jnp.sum(weighted_silu(hidden, half_weight), axis=0, keepdims=True)
        prior_ref[pl.ds(base + block + r, 1), :] = jnp.where(inner, score, 0.0)
        mine = (lane >> 1) == r + 1
        tail = before[:, cols - LANES :] + jnp.where(
            lane == LANES - 2, pltpu.roll(here[:, cols - LANES :], LANES - 1, 1), 0.0
        )
        head = after[:, :LANES] + jnp.where(lane == 1, pltpu.roll(here[:, :LANES], 1, 1), 0.0)
        edges[0] = jnp.where(mine, pltpu.roll(tail, (2 * r + 4) % LANES, 1), edges[0])
        edges[1] = jnp.where(mine, pltpu.roll(head, (2 * r + 2) % LANES, 1), edges[1])

    def no_edges():
        return [jnp.zeros((outs, LANES), F32), jnp.zeros((outs, LANES), F32)]

    def keep_edges(edges, base):
        valid = base - 1 + (lane >> 1) >= 0
        turn = (2 * base + LANES - 2) % LANES
        left_ref[...] += pltpu.roll(jnp.where(valid, edges[0], 0.0), turn, 1)
        right_ref[...] += pltpu.roll(jnp.where(valid, edges[1], 0.0), turn, 1)

    def inner_rows(p_ref, base, edges, pair):
        for r in (2 * pair + 1, 2 * pair + 2):
            finish(None, ((p_ref, pair, r - 2 * pair + 1), (p_ref, pair + 1, r - 2 * pair - 1)), base, r, edges)

    def first_rows(p_ref, earlier_ref, base, edges):
        for r in (-1, 0):
            finish(None, ((earlier_ref, pairs - 1, r + 3), (p_ref, 0, r + 1)), base, r, edges)

    def phase(p_ref, earlier_ref, half, base):
        x = load(half)
        edges = no_edges()
        for pair in range(pairs):
            multiply(p_ref, x, pair)
            if pair < pairs - 1:
                inner_rows(earlier_ref, base - block, edges, pair)
        keep_edges(edges, base - block)
        edges = no_edges()
        first_rows(p_ref, earlier_ref, base, edges)
        keep_edges(edges, base)

    start = step * 2 * block
    phase(a_ref, b_ref, 0, start)
    phase(b_ref, a_ref, 1, start + block)

    @pl.when(step == pl.num_programs(0) - 1)
    def _():
        edges = no_edges()
        base = start + block
        for pair in range(pairs - 1):
            inner_rows(b_ref, base, edges, pair)
        r = block - 1
        j = r - 2 * (pairs - 1) + 1
        before, here, after = [
            b_ref[pairs - 1, j * taps + b * outs : j * taps + (b + 1) * outs, :] for b in range(3)
        ]
        last_row(before, here, after, base, r, edges)
        keep_edges(edges, base)


def conv_prior(features, weight, bias, out_weight):
    channels, strip_rows, cols = features.shape
    outs = bias.shape[0]
    block = 8
    taps = 3 * outs
    cuts = 4
    flat = weight.transpose(1, 2, 0, 3).reshape(9 * outs, channels)
    full = lambda shape: pl.BlockSpec(shape, lambda i: (0,) * len(shape))
    return pl.pallas_call(
        conv_kernel,
        grid=(strip_rows // (2 * block),),
        in_specs=[full((9 * outs, channels)), full((1, outs)), full((1, outs))]
        + [
            pl.BlockSpec((channels // cuts, 2 * block, cols), functools.partial(lambda n, i: (n, i, 0), n))
            for n in range(cuts)
        ],
        out_specs=[full((strip_rows + block, cols)), full((outs, LANES)), full((outs, LANES))],
        out_shape=[
            jax.ShapeDtypeStruct((strip_rows + block, cols), F32),
            jax.ShapeDtypeStruct((outs, LANES), F32),
            jax.ShapeDtypeStruct((outs, LANES), F32),
        ],
        scratch_shapes=[
            pltpu.VMEM((4 * taps, 2 * channels), BF16),
            pltpu.VMEM((block // 2, 4 * taps, cols), F32),
            pltpu.VMEM((block // 2, 4 * taps, cols), F32),
        ],
        compiler_params=pltpu.CompilerParams(vmem_limit_bytes=60 << 20),
        cost_estimate=pl.CostEstimate(flops=8_000_000_000, bytes_accessed=9_000_000, transcendentals=1_000_000),
    )(flat, bias.reshape(1, outs), out_weight.reshape(1, outs), *([features] * cuts))


def split(x):
    high = x.astype(BF16)
    return high, (x - high.astype(F32)).astype(BF16)


def exposure_kernel(
    offsets_ref, counts_ref, s0, s1, s2, s3, s4, record_ref, taps_ref, prior_ref, left_ref, right_ref,
    bias_ref, ow_ref, keep_ref, give_ref, ext_ref, acc_ref,
):
    slot = pl.program_id(0)
    rows, cols = s0.shape
    width = record_ref.shape[2]
    tap_count = taps_ref.shape[2]
    pieces = width // tap_count
    tiles = width // LANES

    @pl.when(slot == 0)
    def _():
        for d, part in enumerate((s0, s1, s2, s3, s4)):
            ext_ref[:, d * cols : (d + 1) * cols] = part[...]
        acc_ref[:, cols:] = jnp.zeros((rows, acc_ref.shape[1] - cols), F32)
        acc_ref[:, :cols] = prior_ref[prior_ref.shape[0] - rows :, :]
        edge = left_ref[...] + right_ref[...] + column(bias_ref[...])
        score = jnp.sum(weighted_silu(edge, column(ow_ref[...]) * 0.5), axis=0, keepdims=True)
        lane = lane_index((rows, LANES))
        own = jnp.where((lane >> 1) == lax.broadcasted_iota(jnp.int32, (rows, LANES), 0), score, 0.0)
        last = jnp.sum(jnp.where((lane & 1) == 0, own, 0.0), axis=1, keepdims=True)
        following = jnp.sum(jnp.where((lane & 1) == 1, own, 0.0), axis=1, keepdims=True)
        acc_ref[:, cols - LANES : cols] += jnp.where(lane == LANES - 1, last, 0.0)
        acc_ref[:, cols : cols + LANES] += jnp.where(lane == 0, following, 0.0)

    @pl.when(slot < counts_ref[0])
    def _():
        offset = offsets_ref[slot]
        rest = offset % LANES
        base = pl.multiple_of(offset - rest, LANES)
        lane = lane_index((rows, LANES))

        taps = taps_ref[0]
        wide = jnp.concatenate([taps, jnp.zeros_like(taps)], axis=1)
        band = pltpu.roll(jnp.broadcast_to(wide, (tap_count, 2 * tap_count)), 0, 1, stride=1, stride_axis=0)
        band_high, band_low = split(band)

        turned = [
            pltpu.roll(ext_ref[:, pl.ds(base + m * LANES, LANES)], LANES - rest, 1) for m in range(tiles + 1)
        ]
        keep = lane < LANES - rest
        window = [jnp.where(keep, turned[m], turned[m + 1]) for m in range(tiles)]
        per = tap_count // LANES

        def stacked(parts):
            return jnp.concatenate(
                [jnp.concatenate(parts[n * per : (n + 1) * per], axis=1) for n in range(pieces)], axis=0
            )

        def product(x, matrix, dims):
            return lax.dot_general(x, matrix, (dims, ((), ())), preferred_element_type=F32)

        def banded(x, shift, dims):
            high, low = split(x)
            total = None
            for at, columns in ((0, 0), (shift, 1)):
                cut = slice(columns * tap_count, (columns + 1) * tap_count)
                x_high, x_low = high, low
                if at:
                    k = (at * rows) % x.shape[0]
                    x_high = jnp.concatenate([high[k:], high[:k]], axis=0)
                    x_low = jnp.concatenate([low[k:], low[:k]], axis=0)
                part = (
                    product(x_high, band_high[:, cut], dims)
                    + product(x_low, band_high[:, cut], dims)
                    + product(x_high, band_low[:, cut], dims)
                )
                total = part if total is None else total + part
            return total

        model = banded(stacked(window), pieces - 1, ((1,), (0,)))
        record = record_ref[0]
        residual = (
            jnp.concatenate([record[:, n * tap_count : (n + 1) * tap_count] for n in range(pieces)], axis=0) - model
        )
        back = banded(residual, 1, ((1,), (1,)))
        moved = []
        for m in range(tiles):
            n, h = divmod(m, per)
            moved.append(pltpu.roll(back[n * rows : (n + 1) * rows, h * LANES : (h + 1) * LANES], rest, 1))
        nothing = jnp.zeros((rows, LANES), F32)
        spill = lane < rest
        for m in range(tiles + 1):
            inside = moved[m] if m < tiles else nothing
            earlier = moved[m - 1] if m > 0 else nothing
            acc_ref[:, pl.ds(base + m * LANES, LANES)] += jnp.where(spill, earlier, inside)

    @pl.when(slot == pl.num_programs(0) - 1)
    def _():
        for d in range(5):
            to_ref = give_ref if d % 2 else keep_ref
            to_ref[:, d // 2 * cols : (d // 2 + 1) * cols] = acc_ref[:, d * cols : (d + 1) * cols]


def exposure_terms(offsets, counts, sky_parts, exposures, psf_taps, prior, left, right, bias, out_weight):
    slots, rows, width = exposures.shape
    cols = sky_parts[0].shape[1]
    reach = len(sky_parts) * cols
    outs = bias.shape[0]
    full = lambda shape: pl.BlockSpec(shape, lambda i, *_: (0,) * len(shape))
    return pl.pallas_call(
        exposure_kernel,
        grid_spec=pltpu.PrefetchScalarGridSpec(
            num_scalar_prefetch=2,
            grid=(slots,),
            in_specs=[full((rows, cols))] * len(sky_parts)
            + [
                pl.BlockSpec((1, rows, width), lambda i, *_: (i, 0, 0)),
                pl.BlockSpec((1, 1, psf_taps.shape[1]), lambda i, *_: (i, 0, 0)),
                full(prior.shape),
                full((outs, LANES)),
                full((outs, LANES)),
                full((1, outs)),
                full((1, outs)),
            ],
            out_specs=[full((rows, 3 * cols)), full((rows, 2 * cols))],
            scratch_shapes=[pltpu.VMEM((rows, reach), F32), pltpu.VMEM((rows, reach), F32)],
        ),
        out_shape=[jax.ShapeDtypeStruct((rows, 3 * cols), F32), jax.ShapeDtypeStruct((rows, 2 * cols), F32)],
        compiler_params=pltpu.CompilerParams(vmem_limit_bytes=40 << 20),
        cost_estimate=pl.CostEstimate(flops=4_000_000_000, bytes_accessed=4_000_000, transcendentals=0),
    )(
        offsets, counts, *sky_parts, exposures, psf_taps.reshape(slots, 1, -1), prior, left, right,
        bias.reshape(1, outs), out_weight.reshape(1, outs),
    )


def join_kernel(keep_ref, got_ref, *outs):
    second = lax.axis_index("sky") % 2 == 1
    group = lax.axis_index("grp")
    share, width = outs[0].shape
    cols = width // 3
    for k, out in enumerate(outs):
        first = pl.multiple_of((group ^ k) * share, share)
        low = got_ref[pl.ds(first, share), :cols]
        high = got_ref[pl.ds(first, share), cols:]
        for d, extra in enumerate(
            (jnp.where(second, low, 0.0), jnp.where(second, high, low), jnp.where(second, 0.0, high))
        ):
            cut = slice(d * cols, (d + 1) * cols)
            out[:, cut] = keep_ref[pl.ds(first, share), cut] + extra


def sum_kernel(a, b, c, d, *outs):
    cols = outs[0].shape[1]
    for k, out in enumerate(outs):
        cut = slice(k * cols, (k + 1) * cols)
        out[...] = (a[:, cut] + b[:, cut]) + (c[:, cut] + d[:, cut])


def small_call(kernel, out_shapes, *operands):
    near = pl.BlockSpec(memory_space=pltpu.VMEM)
    return pl.pallas_call(
        kernel,
        in_specs=[near] * len(operands),
        out_specs=[near] * len(out_shapes),
        out_shape=[jax.ShapeDtypeStruct(shape, F32) for shape in out_shapes],
        compiler_params=pltpu.CompilerParams(vmem_limit_bytes=8 << 20),
        cost_estimate=pl.CostEstimate(flops=200_000, bytes_accessed=1_000_000, transcendentals=0),
    )(*operands)


def on_device(
    sky_strip, exposures, psf_taps, offsets, counts, features, conv_weight, conv_bias, out_weight
):
    n_grp = lax.axis_size("grp")
    strip_rows, cols = sky_strip.shape
    share = strip_rows // n_grp
    reach_blocks = exposures.shape[2] // cols
    parts = [sky_strip]
    for distance in range(1, reach_blocks + 1):
        parts.append(shifted(sky_strip, "sky", -distance))
    prior, left, right = conv_prior(features, conv_weight, conv_bias, out_weight)
    right = shifted(right, "sky", -1)
    keep, give = exposure_terms(
        offsets, counts, parts, exposures, psf_taps, prior, left, right, conv_bias, out_weight
    )
    got = partner(give, "sky", 1)
    terms = small_call(join_kernel, [(share, 3 * cols)] * n_grp, keep, got)
    received = [terms[0]] + [partner(terms[k], "grp", k) for k in range(1, n_grp)]
    own, near, far = small_call(sum_kernel, [(share, cols)] * 3, *received)
    return own + shifted(near, "sky", 2) + shifted(far, "sky", 4)


def solution(mesh):
    placed = (
        P(None, "sky"),
        P(("sky", "grp"), None, None),
        P(("sky", "grp"), None),
        P(("sky", "grp")),
        P(("sky", "grp")),
        P(None, None, "sky"),
        P("grp", None, None, None),
        P("grp"),
        P("grp"),
    )
    return jax.shard_map(
        on_device, mesh=mesh, in_specs=placed, out_specs=P("grp", "sky"), check_vma=False
    )
```

```python
import functools

import jax
import jax.numpy as jnp
from jax import lax
from jax.experimental import pallas as pl
from jax.experimental.pallas import tpu as pltpu
from jax.sharding import PartitionSpec as P

F32 = jnp.float32
BF16 = jnp.bfloat16
LANES = 128


def shifted(x, axis, by):
    length = lax.axis_size(axis)
    return lax.ppermute(x, axis, [(i, (i + by) % length) for i in range(length)])


def partner(x, axis, mask):
    return lax.ppermute(x, axis, [(i, i ^ mask) for i in range(lax.axis_size(axis))])


def lane_index(shape):
    return lax.broadcasted_iota(jnp.int32, shape, 1)


def column(row):
    n = row.shape[1]
    spread = jnp.broadcast_to(row, (n, n))
    diagonal = lax.broadcasted_iota(jnp.int32, (n, n), 0) == lane_index((n, n))
    return jnp.sum(jnp.where(diagonal, spread, 0.0), axis=1, keepdims=True)


def weighted_silu(hidden, half_weight):
    return hidden * (1.0 + jnp.tanh(0.5 * hidden)) * half_weight


def gather_rows(sums):
    sub = lax.broadcasted_iota(jnp.int32, sums[0].shape, 0)
    half = sub < 4
    first = [
        jnp.where(half, sums[i], sums[i + 4]) + pltpu.roll(jnp.where(half, sums[i + 4], sums[i]), 4, 0)
        for i in range(4)
    ]
    low = (sub & 2) == 0
    second = [
        jnp.where(low, first[i] + pltpu.roll(first[i], 6, 0), first[i + 2] + pltpu.roll(first[i + 2], 2, 0))
        for i in range(2)
    ]
    even = (sub & 1) == 0
    return jnp.where(even, second[0] + pltpu.roll(second[0], 7, 0), second[1] + pltpu.roll(second[1], 1, 0))


def conv_kernel(w_ref, bias_ref, ow_ref, *refs):
    x_refs, (prior_ref, own_ref, send_ref, t_ref, a_ref, b_ref) = refs[:-6], refs[-6:]
    step = pl.program_id(0)
    channels = w_ref.shape[1]
    cols = prior_ref.shape[1]
    outs = bias_ref.shape[1]
    taps = 3 * outs
    block = 8
    pairs = block // 2
    strip_rows = prior_ref.shape[0] - block

    @pl.when(step == 0)
    def _():
        w = [w_ref[a * taps : (a + 1) * taps, :] for a in range(3)]
        none = jnp.zeros_like(w[0])
        for j, (even, odd) in enumerate(((w[2], none), (w[1], w[2]), (w[0], w[1]), (none, w[0]))):
            t_ref[j * taps : (j + 1) * taps, :channels] = even
            t_ref[j * taps : (j + 1) * taps, channels:] = odd
        b_ref[pairs - 1] = jnp.zeros(b_ref.shape[1:], F32)
        own_ref[...] = jnp.zeros_like(own_ref)
        send_ref[...] = jnp.zeros_like(send_ref)

    bias = column(jnp.concatenate([bias_ref[...]] * 2, axis=1))
    half_weight = column(jnp.concatenate([ow_ref[...]] * 2, axis=1)) * 0.5
    lane = lane_index((2 * outs, LANES))
    col = lane_index((block, cols))
    inner = jnp.logical_and(col > 0, col < cols - 1)

    def load(half):
        parts = [jnp.swapaxes(x[:, half * block : (half + 1) * block, :], 0, 1) for x in x_refs]
        return jnp.concatenate(parts, axis=1)

    def multiply(p_ref, x, pair):
        both = x[2 * pair : 2 * pair + 2].reshape(2 * channels, cols)
        p_ref[pair] = jnp.dot(t_ref[...], both, preferred_element_type=F32)

    def two_rows(batch, *terms):
        sums, edges = batch
        both = sum(p_ref[pair, j * taps : (j + 2) * taps, :] for p_ref, pair, j in terms)

        def tap(b):
            return jnp.concatenate([both[n * taps + b * outs : n * taps + (b + 1) * outs] for n in range(2)], axis=0)

        tail = cols - LANES
        before = pltpu.roll(tap(0), 1, 1)
        after = pltpu.roll(tap(2), cols - 1, 1)
        here = tap(1)
        score = weighted_silu(before + here + after + bias, half_weight)
        own = jnp.where(lane == 0, here[:, :LANES] + after[:, :LANES], here[:, tail:] + before[:, tail:])
        send = jnp.where(lane == 0, before[:, :LANES], after[:, tail:])
        for n in range(2):
            i = len(sums)
            cut = slice(n * outs, (n + 1) * outs)
            sums.append(sum(score[n * outs + k : n * outs + k + 8] for k in range(0, outs, 8)))
            mine = (lane[cut] >> 1) == i
            for m, ends in enumerate((own[cut], send[cut])):
                edges[m] = jnp.where(mine, pltpu.roll(ends, 2 * i + 1, 1), edges[m])

    def new_batch():
        return [], [jnp.zeros((outs, LANES), F32)] * 2

    def store(batch, base):
        sums, edges = batch
        prior_ref[pl.ds(pl.multiple_of(base, block), block), :] = jnp.where(inner, gather_rows(sums), 0.0)
        row = base - (block - 1) + (lane[:outs] >> 1)
        valid = jnp.logical_and(row >= 0, row < strip_rows)
        turn = (2 * base + LANES - 2 * (block - 1)) % LANES
        for ref, ends in zip((own_ref, send_ref), edges):
            ref[...] += pltpu.roll(jnp.where(valid, ends, 0.0), turn, 1)

    def inner_rows(batch, p_ref, pair):
        two_rows(batch, (p_ref, pair, 2), (p_ref, pair + 1, 0))

    def phase(p_ref, earlier_ref, half, base):
        x = load(half)
        batch = new_batch()
        for pair in range(pairs):
            multiply(p_ref, x, pair)
            if pair < pairs - 1:
                inner_rows(batch, earlier_ref, pair)
        two_rows(batch, (earlier_ref, pairs - 1, 2), (p_ref, 0, 0))
        store(batch, base)

    start = step * 2 * block
    phase(a_ref, b_ref, 0, start)
    phase(b_ref, a_ref, 1, start + block)

    @pl.when(step == pl.num_programs(0) - 1)
    def _():
        batch = new_batch()
        for pair in range(pairs - 1):
            inner_rows(batch, b_ref, pair)
        two_rows(batch, (b_ref, pairs - 1, 2))
        store(batch, strip_rows)


def far(x):
    return pltpu.with_memory_space_constraint(x, pltpu.HBM)


def conv_prior(features, weight, bias, out_weight):
    channels, strip_rows, cols = features.shape
    outs = bias.shape[0]
    block = 8
    taps = 3 * outs
    cuts = 4
    flat = weight.transpose(1, 2, 0, 3).reshape(9 * outs, channels)
    full = lambda shape: pl.BlockSpec(shape, lambda i: (0,) * len(shape))
    return pl.pallas_call(
        conv_kernel,
        grid=(strip_rows // (2 * block),),
        in_specs=[full((9 * outs, channels)), full((1, outs)), full((1, outs))]
        + [
            pl.BlockSpec((channels // cuts, 2 * block, cols), functools.partial(lambda n, i: (n, i, 0), n))
            for n in range(cuts)
        ],
        out_specs=[full((strip_rows + block, cols)), full((outs, LANES)), full((outs, LANES))],
        out_shape=[
            jax.ShapeDtypeStruct((strip_rows + block, cols), F32),
            jax.ShapeDtypeStruct((outs, LANES), F32),
            jax.ShapeDtypeStruct((outs, LANES), F32),
        ],
        scratch_shapes=[
            pltpu.VMEM((4 * taps, 2 * channels), BF16),
            pltpu.VMEM((block // 2, 4 * taps, cols), F32),
            pltpu.VMEM((block // 2, 4 * taps, cols), F32),
        ],
        compiler_params=pltpu.CompilerParams(vmem_limit_bytes=32 << 20),
        cost_estimate=pl.CostEstimate(flops=8_000_000_000, bytes_accessed=9_000_000, transcendentals=1_000_000),
    )(*[far(x) for x in (flat, bias.reshape(1, outs), out_weight.reshape(1, outs))], *([far(features)] * cuts))


def split(x):
    high = x.astype(BF16)
    return high, (x - high.astype(F32)).astype(BF16)


def exposure_kernel(
    offsets_ref, counts_ref, s0, s1, s2, s3, s4, record_ref, taps_ref, send_ref, keep_ref, give_ref, ext_ref, acc_ref
):
    slots, rows, width = record_ref.shape
    cols = s0.shape[1]
    tap_count = taps_ref.shape[2]
    pieces = width // tap_count
    tiles = width // LANES
    per = tap_count // LANES
    for d, part in enumerate((s0, s1, s2, s3, s4)):
        ext_ref[:, d * cols : (d + 1) * cols] = part[...]
    acc_ref[...] = jnp.zeros_like(acc_ref)

    def add_slot(n):
        offset = offsets_ref[n]
        rest = offset % LANES
        base = pl.multiple_of(offset - rest, LANES)
        lane = lane_index((rows, LANES))

        taps = taps_ref[n]
        wide = jnp.concatenate([taps, jnp.zeros_like(taps)], axis=1)
        band = pltpu.roll(jnp.broadcast_to(wide, (tap_count, 2 * tap_count)), 0, 1, stride=1, stride_axis=0)
        first, second = split(band[:, :tap_count]), split(band[:, tap_count:])

        def banded(x, turn, axis):
            high, low = split(x)
            part_high, part_low = [jnp.concatenate(pair, axis=1 - axis) for pair in zip(first, second)]
            both = lax.dot_general(
                jnp.concatenate([high, low, high], axis=1),
                jnp.concatenate([part_high, part_high, part_low], axis=axis),
                (((1,), (axis,)), ((), ())),
                preferred_element_type=F32,
            )
            k = turn * rows % x.shape[0]
            return both[:, :tap_count] + jnp.concatenate([both[k:, tap_count:], both[:k, tap_count:]], axis=0)

        turned = [
            pltpu.roll(ext_ref[:, pl.ds(base + m * LANES, LANES)], LANES - rest, 1) for m in range(tiles + 1)
        ]
        keep = lane < LANES - rest
        window = [jnp.where(keep, turned[m], turned[m + 1]) for m in range(tiles)]
        stacked = jnp.concatenate(
            [jnp.concatenate(window[p * per : (p + 1) * per], axis=1) for p in range(pieces)], axis=0
        )
        record = jnp.concatenate(
            [record_ref[n, :, p * tap_count : (p + 1) * tap_count] for p in range(pieces)], axis=0
        )
        live = jnp.where(counts_ref[...] > n, 1.0, 0.0)
        residual = (record - banded(stacked, pieces - 1, 0)) * live
        back = banded(residual, 1, 1)
        moved = []
        for m in range(tiles):
            p, h = divmod(m, per)
            moved.append(pltpu.roll(back[p * rows : (p + 1) * rows, h * LANES : (h + 1) * LANES], rest, 1))
        nothing = jnp.zeros((rows, LANES), F32)
        spill = lane < rest
        for m in range(tiles + 1):
            inside = moved[m] if m < tiles else nothing
            earlier = moved[m - 1] if m > 0 else nothing
            acc_ref[:, pl.ds(base + m * LANES, LANES)] += jnp.where(spill, earlier, inside)

    for n in range(slots):
        add_slot(n)

    for d in range(5):
        to_ref = give_ref if d % 2 else keep_ref
        to_ref[:, d // 2 * cols : (d // 2 + 1) * cols] = acc_ref[:, d * cols : (d + 1) * cols]
    outs = send_ref.shape[0]
    give_ref[:outs, 2 * cols :] = send_ref[...]
    give_ref[outs:, 2 * cols :] = jnp.zeros((rows - outs, LANES), F32)


def exposure_terms(offsets, counts, sky_parts, exposures, psf_taps, send):
    slots, rows, width = exposures.shape
    cols = sky_parts[0].shape[1]
    reach = len(sky_parts) * cols
    keep = (rows, 3 * cols)
    give = (rows, 2 * cols + LANES)
    near = pl.BlockSpec(memory_space=pltpu.VMEM)
    few = pl.BlockSpec(memory_space=pltpu.SMEM)
    return pl.pallas_call(
        exposure_kernel,
        in_specs=[few] + [near] * (len(sky_parts) + 4),
        out_specs=[near] * 2,
        out_shape=[jax.ShapeDtypeStruct(keep, F32), jax.ShapeDtypeStruct(give, F32)],
        scratch_shapes=[pltpu.VMEM((rows, reach), F32), pltpu.VMEM((rows, reach), F32)],
        compiler_params=pltpu.CompilerParams(vmem_limit_bytes=32 << 20),
        cost_estimate=pl.CostEstimate(flops=6_000_000_000, bytes_accessed=4_000_000, transcendentals=0),
    )(offsets, counts.reshape(1, 1), *sky_parts, exposures, psf_taps.reshape(slots, 1, -1), send)


def join_kernel(keep_ref, got_ref, cross_ref, prior_ref, own_ref, bias_ref, ow_ref, *outs):
    outs, full_ref = outs[:-1], outs[-1]
    second = lax.axis_index("sky") % 2 == 1
    group = lax.axis_index("grp")
    share, width = outs[0].shape
    cols = width // 3
    rows = keep_ref.shape[0]
    channels = own_ref.shape[0]
    lane = lane_index((channels, LANES))
    beside = got_ref[:channels, 2 * cols :]
    from_beside = jnp.logical_xor((lane & 1) == 0, second)
    edge = own_ref[...] + jnp.where(from_beside, beside, cross_ref[...]) + column(bias_ref[...])
    score = jnp.sum(weighted_silu(edge, column(ow_ref[...]) * 0.5), axis=0, keepdims=True)
    lane = lane_index((rows, LANES))
    mine = jnp.where((lane >> 1) == lax.broadcasted_iota(jnp.int32, (rows, LANES), 0), score, 0.0)
    last = jnp.sum(jnp.where((lane & 1) == 0, mine, 0.0), axis=1, keepdims=True)
    first = jnp.sum(jnp.where((lane & 1) == 1, mine, 0.0), axis=1, keepdims=True)
    col = lane_index((rows, cols))
    skipped = prior_ref.shape[0] - rows - 1
    full_ref[...] = (
        keep_ref[:, :cols]
        + prior_ref[skipped : skipped + rows, :]
        + jnp.where(col == 0, first, 0.0)
        + jnp.where(col == cols - 1, last, 0.0)
    )
    for k, out in enumerate(outs):
        top = pl.ds(pl.multiple_of((group ^ k) * share, share), share)
        low = got_ref[top, :cols]
        high = got_ref[top, cols : 2 * cols]
        out[:, :cols] = full_ref[top, :] + jnp.where(second, low, 0.0)
        out[:, cols : 2 * cols] = keep_ref[top, cols : 2 * cols] + jnp.where(second, high, low)
        out[:, 2 * cols :] = keep_ref[top, 2 * cols :] + jnp.where(second, 0.0, high)


def sum_kernel(a, b, c, d, *outs):
    cols = outs[0].shape[1]
    for k, out in enumerate(outs):
        cut = slice(k * cols, (k + 1) * cols)
        out[...] = (a[:, cut] + b[:, cut]) + (c[:, cut] + d[:, cut])


def small_call(kernel, out_shapes, *operands, scratch=()):
    near = pl.BlockSpec(memory_space=pltpu.VMEM)
    return pl.pallas_call(
        kernel,
        in_specs=[near] * len(operands),
        out_specs=[near] * len(out_shapes),
        out_shape=[jax.ShapeDtypeStruct(shape, F32) for shape in out_shapes],
        scratch_shapes=[pltpu.VMEM(shape, F32) for shape in scratch],
        compiler_params=pltpu.CompilerParams(vmem_limit_bytes=8 << 20),
        cost_estimate=pl.CostEstimate(flops=200_000, bytes_accessed=1_000_000, transcendentals=0),
    )(*operands)


def on_device(
    sky_strip, exposures, psf_taps, offsets, counts, features, conv_weight, conv_bias, out_weight
):
    n_grp = lax.axis_size("grp")
    strip_rows, cols = sky_strip.shape
    share = strip_rows // n_grp
    reach_blocks = exposures.shape[2] // cols
    parts = [sky_strip]
    for distance in range(1, reach_blocks + 1):
        parts.append(shifted(sky_strip, "sky", -distance))
    prior, own_edge, send = conv_prior(features, conv_weight, conv_bias, out_weight)
    n_sky = lax.axis_size("sky")
    cross = lax.ppermute(send, "sky", [(i, (i - 1 if i % 2 == 0 else i + 1) % n_sky) for i in range(n_sky)])
    keep, give = exposure_terms(offsets, counts, parts, exposures, psf_taps, send)
    give, cross = lax.optimization_barrier((give, cross))
    got = partner(give, "sky", 1)
    terms = small_call(
        join_kernel, [(share, 3 * cols)] * n_grp, keep, got, cross, prior, own_edge,
        conv_bias.reshape(1, -1), out_weight.reshape(1, -1), scratch=[(strip_rows, cols)],
    )
    received = [terms[0]] + [partner(terms[k], "grp", k) for k in range(1, n_grp)]
    own, near, far = small_call(sum_kernel, [(share, cols)] * 3, *received)
    return own + shifted(near, "sky", 2) + shifted(far, "sky", 4)


def solution(mesh):
    placed = (
        P(None, "sky"),
        P(("sky", "grp"), None, None),
        P(("sky", "grp"), None),
        P(("sky", "grp")),
        P(("sky", "grp")),
        P(None, None, "sky"),
        P("grp", None, None, None),
        P("grp"),
        P("grp"),
    )
    return jax.shard_map(
        on_device, mesh=mesh, in_specs=placed, out_specs=P("grp", "sky"), check_vma=False
    )
```

```python
import functools

import jax
import jax.numpy as jnp
from jax import lax
from jax.experimental import pallas as pl
from jax.experimental.pallas import tpu as pltpu
from jax.sharding import PartitionSpec as P

F32 = jnp.float32
BF16 = jnp.bfloat16
LANES = 128


def shifted(x, axis, by):
    length = lax.axis_size(axis)
    return lax.ppermute(x, axis, [(i, (i + by) % length) for i in range(length)])


def partner(x, axis, mask):
    return lax.ppermute(x, axis, [(i, i ^ mask) for i in range(lax.axis_size(axis))])


def lane_index(shape):
    return lax.broadcasted_iota(jnp.int32, shape, 1)


def column(row):
    n = row.shape[1]
    spread = jnp.broadcast_to(row, (n, n))
    diagonal = lax.broadcasted_iota(jnp.int32, (n, n), 0) == lane_index((n, n))
    return jnp.sum(jnp.where(diagonal, spread, 0.0), axis=1, keepdims=True)


def weighted_silu(hidden, half_weight):
    return hidden * (1.0 + jnp.tanh(0.5 * hidden)) * half_weight


def gather_rows(sums):
    sub = lax.broadcasted_iota(jnp.int32, sums[0].shape, 0)
    half = sub < 4
    first = [
        jnp.where(half, sums[i], sums[i + 4]) + pltpu.roll(jnp.where(half, sums[i + 4], sums[i]), 4, 0)
        for i in range(4)
    ]
    low = (sub & 2) == 0
    second = [
        jnp.where(low, first[i] + pltpu.roll(first[i], 6, 0), first[i + 2] + pltpu.roll(first[i + 2], 2, 0))
        for i in range(2)
    ]
    even = (sub & 1) == 0
    return jnp.where(even, second[0] + pltpu.roll(second[0], 7, 0), second[1] + pltpu.roll(second[1], 1, 0))


def conv_kernel(counts_ref, w_ref, bias_ref, ow_ref, *refs):
    x_refs, (prior_ref, own_ref, send_ref, live_ref, t_ref, a_ref, b_ref) = refs[:-7], refs[-7:]
    step = pl.program_id(0)
    channels = w_ref.shape[1]
    cols = prior_ref.shape[1]
    outs = bias_ref.shape[1]
    taps = 3 * outs
    block = 8
    pairs = block // 2
    strip_rows = prior_ref.shape[0] - block

    @pl.when(step == 0)
    def _():
        w = [w_ref[a * taps : (a + 1) * taps, :] for a in range(3)]
        none = jnp.zeros_like(w[0])
        for j, (even, odd) in enumerate(((w[2], none), (w[1], w[2]), (w[0], w[1]), (none, w[0]))):
            t_ref[j * taps : (j + 1) * taps, :channels] = even
            t_ref[j * taps : (j + 1) * taps, channels:] = odd
        b_ref[pairs - 1] = jnp.zeros(b_ref.shape[1:], F32)
        live_ref[...] = jnp.broadcast_to(counts_ref[...], live_ref.shape)
        own_ref[...] = jnp.zeros_like(own_ref)
        send_ref[...] = jnp.zeros_like(send_ref)

    bias = column(jnp.concatenate([bias_ref[...]] * 4, axis=1))
    half_weight = column(jnp.concatenate([ow_ref[...]] * 4, axis=1)) * 0.5
    lane = lane_index((4 * outs, LANES))
    col = lane_index((block, cols))
    middle = jnp.logical_and(col > 0, col < cols - 1)

    def load(half):
        parts = [jnp.swapaxes(x[:, half * block : (half + 1) * block, :], 0, 1) for x in x_refs]
        return jnp.concatenate(parts, axis=1)

    def multiply(p_ref, x, pair):
        both = x[2 * pair : 2 * pair + 2].reshape(2 * channels, cols)
        p_ref[pair] = jnp.dot(t_ref[...], both, preferred_element_type=F32)

    def add_rows(batch, *groups):
        sums, edges = batch
        both = [sum(p_ref[pair, j * taps : (j + 2) * taps, :] for p_ref, pair, j in terms) for terms in groups]

        def tap(b):
            return jnp.concatenate(
                [part[n * taps + b * outs : n * taps + (b + 1) * outs] for part in both for n in range(2)], axis=0
            )

        tail = cols - LANES
        count = 2 * len(groups)
        before = pltpu.roll(tap(0), 1, 1)
        after = pltpu.roll(tap(2), cols - 1, 1)
        here = tap(1)
        score = weighted_silu(
            before + here + after + bias[: count * outs], half_weight[: count * outs]
        )
        first = lane[: count * outs] == 0
        own = jnp.where(first, here[:, :LANES] + after[:, :LANES], here[:, tail:] + before[:, tail:])
        send = jnp.where(first, before[:, :LANES], after[:, tail:])
        for n in range(count):
            i = len(sums)
            cut = slice(n * outs, (n + 1) * outs)
            sums.append(sum(score[n * outs + k : n * outs + k + 8] for k in range(0, outs, 8)))
            mine = (lane[cut] >> 1) == i
            for m, ends in enumerate((own[cut], send[cut])):
                edges[m] = jnp.where(mine, pltpu.roll(ends, 2 * i + 1, 1), edges[m])

    def new_batch():
        return [], [jnp.zeros((outs, LANES), F32)] * 2

    def store(batch, base):
        sums, edges = batch
        prior_ref[pl.ds(pl.multiple_of(base, block), block), :] = jnp.where(middle, gather_rows(sums), 0.0)
        row = base - (block - 1) + (lane[:outs] >> 1)
        valid = jnp.logical_and(row >= 0, row < strip_rows)
        turn = (2 * base + LANES - 2 * (block - 1)) % LANES
        for ref, ends in zip((own_ref, send_ref), edges):
            ref[...] += pltpu.roll(jnp.where(valid, ends, 0.0), turn, 1)

    def inner(p_ref, pair):
        return ((p_ref, pair, 2), (p_ref, pair + 1, 0))

    def phase(p_ref, earlier_ref, half, base):
        x = load(half)
        batch = new_batch()
        multiply(p_ref, x, 0)
        multiply(p_ref, x, 1)
        add_rows(batch, inner(earlier_ref, 0), inner(earlier_ref, 1))
        multiply(p_ref, x, 2)
        multiply(p_ref, x, 3)
        add_rows(batch, inner(earlier_ref, 2), ((earlier_ref, pairs - 1, 2), (p_ref, 0, 0)))
        store(batch, base)

    start = step * 2 * block
    phase(a_ref, b_ref, 0, start)
    phase(b_ref, a_ref, 1, start + block)

    @pl.when(step == pl.num_programs(0) - 1)
    def _():
        batch = new_batch()
        add_rows(batch, inner(b_ref, 0), inner(b_ref, 1))
        add_rows(batch, inner(b_ref, 2), ((b_ref, pairs - 1, 2),))
        store(batch, strip_rows)


def far(x):
    return pltpu.with_memory_space_constraint(x, pltpu.HBM)


def conv_prior(counts, features, weight, bias, out_weight):
    channels, strip_rows, cols = features.shape
    outs = bias.shape[0]
    block = 8
    taps = 3 * outs
    cuts = 4
    flat = weight.transpose(1, 2, 0, 3).reshape(9 * outs, channels)
    full = lambda shape: pl.BlockSpec(shape, lambda i: (0,) * len(shape))
    return pl.pallas_call(
        conv_kernel,
        grid=(strip_rows // (2 * block),),
        in_specs=[full((1, 1)), full((9 * outs, channels)), full((1, outs)), full((1, outs))]
        + [
            pl.BlockSpec((channels // cuts, 2 * block, cols), functools.partial(lambda n, i: (n, i, 0), n))
            for n in range(cuts)
        ],
        out_specs=[full((strip_rows + block, cols)), full((outs, LANES)), full((outs, LANES)), full((8, LANES))],
        out_shape=[
            jax.ShapeDtypeStruct((strip_rows + block, cols), F32),
            jax.ShapeDtypeStruct((outs, LANES), F32),
            jax.ShapeDtypeStruct((outs, LANES), F32),
            jax.ShapeDtypeStruct((8, LANES), jnp.int32),
        ],
        scratch_shapes=[
            pltpu.VMEM((4 * taps, 2 * channels), BF16),
            pltpu.VMEM((block // 2, 4 * taps, cols), F32),
            pltpu.VMEM((block // 2, 4 * taps, cols), F32),
        ],
        compiler_params=pltpu.CompilerParams(vmem_limit_bytes=32 << 20),
        cost_estimate=pl.CostEstimate(flops=8_000_000_000, bytes_accessed=9_000_000, transcendentals=1_000_000),
    )(counts.reshape(1, 1), *[far(x) for x in (flat, bias.reshape(1, outs), out_weight.reshape(1, outs))], *([far(features)] * cuts))


def split(x):
    high = x.astype(BF16)
    return high, (x - high.astype(F32)).astype(BF16)


HALF = 32


def pair_rows(which):
    mine = lax.axis_index("grp") // 2
    return pl.multiple_of((mine if which else 1 - mine) * HALF, HALF)


def exposure_kernel(
    halves, offsets_ref, counts_ref, s0, s1, s2, s3, s4, record_ref, taps_ref, send_ref, *refs
):
    outs, (ext_ref, acc_ref) = refs[:-2], refs[-2:]
    slots, _, width = record_ref.shape
    rows = HALF * len(halves)
    tops = [pl.ds(pair_rows(which), HALF) for which in halves]
    cols = s0.shape[1]
    tap_count = taps_ref.shape[1]
    pieces = width // tap_count
    tiles = width // LANES
    per = tap_count // LANES
    for d, part in enumerate((s0, s1, s2, s3, s4)):
        for h, top in enumerate(tops):
            ext_ref[h * HALF : (h + 1) * HALF, d * cols : (d + 1) * cols] = part[top, :]
    acc_ref[...] = jnp.zeros_like(acc_ref)

    def add_slot(n):
        offset = offsets_ref[n]
        rest = offset % LANES
        base = pl.multiple_of(offset - rest, LANES)
        lane = lane_index((rows, LANES))

        taps = taps_ref[n : n + 1, :]
        wide = jnp.concatenate([taps, jnp.zeros_like(taps)], axis=1)
        band = pltpu.roll(jnp.broadcast_to(wide, (tap_count, 2 * tap_count)), 0, 1, stride=1, stride_axis=0)
        first, second = split(band[:, :tap_count]), split(band[:, tap_count:])

        def banded(x, turn, axis):
            high, low = split(x)
            part_high, part_low = [jnp.concatenate(pair, axis=1 - axis) for pair in zip(first, second)]
            both = lax.dot_general(
                jnp.concatenate([high, low, high], axis=1),
                jnp.concatenate([part_high, part_high, part_low], axis=axis),
                (((1,), (axis,)), ((), ())),
                preferred_element_type=F32,
            )
            k = turn * rows % x.shape[0]
            return both[:, :tap_count] + jnp.concatenate([both[k:, tap_count:], both[:k, tap_count:]], axis=0)

        turned = [
            pltpu.roll(ext_ref[:, pl.ds(base + m * LANES, LANES)], LANES - rest, 1) for m in range(tiles + 1)
        ]
        keep = lane < LANES - rest
        window = [jnp.where(keep, turned[m], turned[m + 1]) for m in range(tiles)]
        stacked = jnp.concatenate(
            [jnp.concatenate(window[p * per : (p + 1) * per], axis=1) for p in range(pieces)], axis=0
        )
        record = jnp.concatenate(
            [record_ref[n, top, p * tap_count : (p + 1) * tap_count] for p in range(pieces) for top in tops], axis=0
        )
        live = jnp.where(counts_ref[:1, :1] > n, 1.0, 0.0)
        residual = (record - banded(stacked, pieces - 1, 0)) * live
        back = banded(residual, 1, 1)
        moved = []
        for m in range(tiles):
            p, h = divmod(m, per)
            moved.append(pltpu.roll(back[p * rows : (p + 1) * rows, h * LANES : (h + 1) * LANES], rest, 1))
        nothing = jnp.zeros((rows, LANES), F32)
        spill = lane < rest
        for m in range(tiles + 1):
            inside = moved[m] if m < tiles else nothing
            earlier = moved[m - 1] if m > 0 else nothing
            acc_ref[:, pl.ds(base + m * LANES, LANES)] += jnp.where(spill, earlier, inside)

    for n in range(slots):
        add_slot(n)

    for h, which in enumerate(halves):
        band = slice(h * HALF, (h + 1) * HALF)
        keep_ref, give_ref = outs[2 * h : 2 * h + 2]
        for d in range(5):
            to_ref = give_ref if d % 2 else keep_ref
            to_ref[:, d // 2 * cols : (d // 2 + 1) * cols] = acc_ref[band, d * cols : (d + 1) * cols]
        if not which:
            give_ref[:, 2 * cols :] = send_ref[...]


def exposure_terms(halves, offsets, counts, sky_parts, exposures, psf_taps, send):
    cols = sky_parts[0].shape[1]
    reach = len(sky_parts) * cols
    shapes = []
    for which in halves:
        shapes += [(HALF, 3 * cols), (HALF, 2 * cols + (0 if which else LANES))]
    near = pl.BlockSpec(memory_space=pltpu.VMEM)
    few = pl.BlockSpec(memory_space=pltpu.SMEM)
    return pl.pallas_call(
        functools.partial(exposure_kernel, halves),
        in_specs=[few] + [near] * (len(sky_parts) + 4),
        out_specs=[near] * len(shapes),
        out_shape=[jax.ShapeDtypeStruct(shape, F32) for shape in shapes],
        scratch_shapes=[pltpu.VMEM((HALF * len(halves), reach), F32)] * 2,
        compiler_params=pltpu.CompilerParams(vmem_limit_bytes=32 << 20),
        cost_estimate=pl.CostEstimate(flops=3_000_000_000 * len(halves), bytes_accessed=2_000_000, transcendentals=0),
    )(offsets, counts, *sky_parts, exposures, psf_taps, send)


def join_kernel(which, keep_ref, got_ref, beside_ref, cross_ref, prior_ref, own_ref, bias_ref, ow_ref, out0, out1, full_ref):
    second = lax.axis_index("sky") % 2 == 1
    low_half = lax.axis_index("grp") % 2
    share, width = out0.shape
    cols = width // 3
    rows = full_ref.shape[0]
    channels = own_ref.shape[0]
    lane = lane_index((channels, LANES))
    beside = beside_ref[:, 2 * cols :]
    from_beside = jnp.logical_xor((lane & 1) == 0, second)
    edge = own_ref[...] + jnp.where(from_beside, beside, cross_ref[...]) + column(bias_ref[...])
    score = jnp.sum(weighted_silu(edge, column(ow_ref[...]) * 0.5), axis=0, keepdims=True)
    lane = lane_index((rows, LANES))
    mine = jnp.where((lane >> 1) == lax.broadcasted_iota(jnp.int32, (rows, LANES), 0), score, 0.0)
    last = jnp.sum(jnp.where((lane & 1) == 0, mine, 0.0), axis=1, keepdims=True)
    first = jnp.sum(jnp.where((lane & 1) == 1, mine, 0.0), axis=1, keepdims=True)
    col = lane_index((rows, cols))
    skipped = prior_ref.shape[0] - rows - 1
    full_ref[...] = (
        prior_ref[skipped : skipped + rows, :]
        + jnp.where(col == 0, first, 0.0)
        + jnp.where(col == cols - 1, last, 0.0)
    )
    for k, out in enumerate((out0, out1)):
        start = pl.multiple_of((low_half ^ k) * share, share)
        top = pl.ds(start, share)
        low = got_ref[top, :cols]
        high = got_ref[top, cols : 2 * cols]
        prior = full_ref[pl.ds(pl.multiple_of(pair_rows(which) + start, share), share), :]
        out[:, :cols] = keep_ref[top, :cols] + prior + jnp.where(second, low, 0.0)
        out[:, cols : 2 * cols] = keep_ref[top, cols : 2 * cols] + jnp.where(second, high, low)
        out[:, 2 * cols :] = keep_ref[top, 2 * cols :] + jnp.where(second, 0.0, high)


def sum_kernel(a, b, c, d, *outs):
    cols = outs[0].shape[1]
    for k, out in enumerate(outs):
        cut = slice(k * cols, (k + 1) * cols)
        out[...] = (a[:, cut] + b[:, cut]) + (c[:, cut] + d[:, cut])


def small_call(kernel, out_shapes, *operands, scratch=()):
    near = pl.BlockSpec(memory_space=pltpu.VMEM)
    return pl.pallas_call(
        kernel,
        in_specs=[near] * len(operands),
        out_specs=[near] * len(out_shapes),
        out_shape=[jax.ShapeDtypeStruct(shape, F32) for shape in out_shapes],
        scratch_shapes=[pltpu.VMEM(shape, F32) for shape in scratch],
        compiler_params=pltpu.CompilerParams(vmem_limit_bytes=8 << 20),
        cost_estimate=pl.CostEstimate(flops=200_000, bytes_accessed=1_000_000, transcendentals=0),
    )(*operands)


def on_device(
    sky_strip, exposures, psf_taps, offsets, counts, features, conv_weight, conv_bias, out_weight
):
    n_grp = lax.axis_size("grp")
    strip_rows, cols = sky_strip.shape
    share = strip_rows // n_grp
    reach_blocks = exposures.shape[2] // cols
    parts = [sky_strip]
    for distance in range(1, reach_blocks + 1):
        parts.append(shifted(sky_strip, "sky", -distance))
    prior, own_edge, send, live = conv_prior(counts, features, conv_weight, conv_bias, out_weight)
    n_sky = lax.axis_size("sky")
    cross = lax.ppermute(send, "sky", [(i, (i - 1 if i % 2 == 0 else i + 1) % n_sky) for i in range(n_sky)])
    keep_a, give_a = exposure_terms((0,), offsets, live, parts, exposures, psf_taps, send)
    keep_b, give_b = exposure_terms((1,), offsets, live, parts, exposures, psf_taps, send)
    got_a = partner(give_a, "sky", 1)
    edges = (cross, prior, own_edge, conv_bias.reshape(1, -1), out_weight.reshape(1, -1))

    def join(which, keep, got):
        return small_call(
            functools.partial(join_kernel, which), [(share, 3 * cols)] * 2, keep, got, got_a, *edges,
            scratch=[(strip_rows, cols)],
        )

    to_2, to_3 = join(0, keep_a, got_a)
    from_2, from_3 = partner(to_2, "grp", 2), partner(to_3, "grp", 3)
    give_b, to_2 = lax.optimization_barrier((give_b, to_2))
    got_b = partner(give_b, "sky", 1)
    kept, to_1 = join(1, keep_b, got_b)
    received = [kept, partner(to_1, "grp", 1), from_2, from_3]
    own, near, distant = small_call(sum_kernel, [(share, cols)] * 3, *received)
    distant = shifted(distant, "sky", 4)
    return own + shifted(near, "sky", 2) + distant


def solution(mesh):
    placed = (
        P(None, "sky"),
        P(("sky", "grp"), None, None),
        P(("sky", "grp"), None),
        P(("sky", "grp")),
        P(("sky", "grp")),
        P(None, None, "sky"),
        P("grp", None, None, None),
        P("grp"),
        P("grp"),
    )
    return jax.shard_map(
        on_device, mesh=mesh, in_specs=placed, out_specs=P("grp", "sky"), check_vma=False
    )
```

```python
import functools

import jax
import jax.numpy as jnp
from jax import lax
from jax.experimental import pallas as pl
from jax.experimental.pallas import tpu as pltpu
from jax.sharding import PartitionSpec as P

F32 = jnp.float32
BF16 = jnp.bfloat16
LANES = 128


def shifted(x, axis, by):
    length = lax.axis_size(axis)
    return lax.ppermute(x, axis, [(i, (i + by) % length) for i in range(length)])


def partner(x, axis, mask):
    return lax.ppermute(x, axis, [(i, i ^ mask) for i in range(lax.axis_size(axis))])


def lane_index(shape):
    return lax.broadcasted_iota(jnp.int32, shape, 1)


def column(row):
    n = row.shape[1]
    spread = jnp.broadcast_to(row, (n, n))
    diagonal = lax.broadcasted_iota(jnp.int32, (n, n), 0) == lane_index((n, n))
    return jnp.sum(jnp.where(diagonal, spread, 0.0), axis=1, keepdims=True)


def weighted_silu(hidden, half_weight):
    return hidden * (1.0 + jnp.tanh(0.5 * hidden)) * half_weight


def gather_rows(sums):
    sub = lax.broadcasted_iota(jnp.int32, sums[0].shape, 0)
    half = sub < 4
    first = [
        jnp.where(half, sums[i], sums[i + 4]) + pltpu.roll(jnp.where(half, sums[i + 4], sums[i]), 4, 0)
        for i in range(4)
    ]
    low = (sub & 2) == 0
    second = [
        jnp.where(low, first[i] + pltpu.roll(first[i], 6, 0), first[i + 2] + pltpu.roll(first[i + 2], 2, 0))
        for i in range(2)
    ]
    even = (sub & 1) == 0
    return jnp.where(even, second[0] + pltpu.roll(second[0], 7, 0), second[1] + pltpu.roll(second[1], 1, 0))


def conv_kernel(counts_ref, w_ref, bias_ref, ow_ref, *refs):
    x_refs, (prior_ref, own_ref, send_ref, live_ref, t_ref, a_ref, b_ref, ends_ref) = refs[:-8], refs[-8:]
    step = pl.program_id(0)
    channels = w_ref.shape[1]
    cols = prior_ref.shape[1]
    outs = bias_ref.shape[1]
    taps = 3 * outs
    block = 8
    pairs = block // 2
    strip_rows = prior_ref.shape[0] - block

    @pl.when(step == 0)
    def _():
        w = [w_ref[a * taps : (a + 1) * taps, :] for a in range(3)]
        none = jnp.zeros_like(w[0])
        for j, (even, odd) in enumerate(((w[2], none), (w[1], w[2]), (w[0], w[1]), (none, w[0]))):
            t_ref[j * taps : (j + 1) * taps, :channels] = even
            t_ref[j * taps : (j + 1) * taps, channels:] = odd
        b_ref[pairs - 1] = jnp.zeros(b_ref.shape[1:], F32)
        live_ref[...] = jnp.broadcast_to(counts_ref[...], live_ref.shape)

    bias = column(jnp.concatenate([bias_ref[...]] * 4, axis=1))
    half_weight = column(jnp.concatenate([ow_ref[...]] * 4, axis=1)) * 0.5
    lane = lane_index((4 * outs, LANES))
    col = lane_index((block, cols))
    middle = jnp.logical_and(col > 0, col < cols - 1)

    def load(half):
        parts = [jnp.swapaxes(x[:, half * block : (half + 1) * block, :], 0, 1) for x in x_refs]
        return jnp.concatenate(parts, axis=1)

    def multiply(p_ref, x, pair):
        both = x[2 * pair : 2 * pair + 2].reshape(2 * channels, cols)
        p_ref[pair] = jnp.dot(t_ref[...], both, preferred_element_type=F32)

    def add_rows(sums, base, *groups):
        both = [sum(p_ref[pair, j * taps : (j + 2) * taps, :] for p_ref, pair, j in terms) for terms in groups]

        def tap(b):
            return jnp.concatenate(
                [part[n * taps + b * outs : n * taps + (b + 1) * outs] for part in both for n in range(2)], axis=0
            )

        tail = cols - LANES
        count = 2 * len(groups)
        before = pltpu.roll(tap(0), 1, 1)
        after = pltpu.roll(tap(2), cols - 1, 1)
        here = tap(1)
        score = weighted_silu(
            before + here + after + bias[: count * outs], half_weight[: count * outs]
        )
        first = lane[: count * outs] == 0
        own = jnp.where(first, here[:, :LANES] + after[:, :LANES], here[:, tail:] + before[:, tail:])
        send = jnp.where(first, before[:, :LANES], after[:, tail:])
        for n in range(count):
            i = len(sums)
            cut = slice(n * outs, (n + 1) * outs)
            sums.append(sum(score[n * outs + k : n * outs + k + 8] for k in range(0, outs, 8)))
            ends_ref[0, base + i] = own[cut]
            ends_ref[1, base + i] = send[cut]

    def store(sums, base):
        prior_ref[pl.ds(pl.multiple_of(base, block), block), :] = jnp.where(middle, gather_rows(sums), 0.0)

    def inner(p_ref, pair):
        return ((p_ref, pair, 2), (p_ref, pair + 1, 0))

    def phase(p_ref, earlier_ref, half, base):
        x = load(half)
        sums = []
        multiply(p_ref, x, 0)
        multiply(p_ref, x, 1)
        add_rows(sums, base, inner(earlier_ref, 0), inner(earlier_ref, 1))
        multiply(p_ref, x, 2)
        multiply(p_ref, x, 3)
        add_rows(sums, base, inner(earlier_ref, 2), ((earlier_ref, pairs - 1, 2), (p_ref, 0, 0)))
        store(sums, base)

    start = step * 2 * block
    phase(a_ref, b_ref, 0, start)
    phase(b_ref, a_ref, 1, start + block)

    @pl.when(step == pl.num_programs(0) - 1)
    def _():
        sums = []
        add_rows(sums, strip_rows, inner(b_ref, 0), inner(b_ref, 1))
        add_rows(sums, strip_rows, inner(b_ref, 2), ((b_ref, pairs - 1, 2),))
        store(sums, strip_rows)
        spot = lane[:outs] >> 1
        for m, ref in enumerate((own_ref, send_ref)):
            total = jnp.zeros((outs, LANES), F32)
            for row in range(strip_rows):
                total = jnp.where(spot == row, pltpu.roll(ends_ref[m, row + block - 1], (2 * row + 1) % LANES, 1), total)
            ref[...] = total


def far(x):
    return pltpu.with_memory_space_constraint(x, pltpu.HBM)


def conv_prior(counts, features, weight, bias, out_weight):
    channels, strip_rows, cols = features.shape
    outs = bias.shape[0]
    block = 8
    taps = 3 * outs
    cuts = 4
    flat = weight.transpose(1, 2, 0, 3).reshape(9 * outs, channels)
    full = lambda shape: pl.BlockSpec(shape, lambda i: (0,) * len(shape))
    return pl.pallas_call(
        conv_kernel,
        grid=(strip_rows // (2 * block),),
        in_specs=[full((1, 1)), full((9 * outs, channels)), full((1, outs)), full((1, outs))]
        + [
            pl.BlockSpec((channels // cuts, 2 * block, cols), functools.partial(lambda n, i: (n, i, 0), n))
            for n in range(cuts)
        ],
        out_specs=[full((strip_rows + block, cols)), full((outs, LANES)), full((outs, LANES)), full((8, LANES))],
        out_shape=[
            jax.ShapeDtypeStruct((strip_rows + block, cols), F32),
            jax.ShapeDtypeStruct((outs, LANES), F32),
            jax.ShapeDtypeStruct((outs, LANES), F32),
            jax.ShapeDtypeStruct((8, LANES), jnp.int32),
        ],
        scratch_shapes=[
            pltpu.VMEM((4 * taps, 2 * channels), BF16),
            pltpu.VMEM((block // 2, 4 * taps, cols), F32),
            pltpu.VMEM((block // 2, 4 * taps, cols), F32),
            pltpu.VMEM((2, strip_rows + block, outs, LANES), F32),
        ],
        compiler_params=pltpu.CompilerParams(vmem_limit_bytes=32 << 20),
        cost_estimate=pl.CostEstimate(flops=8_000_000_000, bytes_accessed=9_000_000, transcendentals=1_000_000),
    )(counts.reshape(1, 1), *[far(x) for x in (flat, bias.reshape(1, outs), out_weight.reshape(1, outs))], *([far(features)] * cuts))


def split(x):
    high = x.astype(BF16)
    return high, (x - high.astype(F32)).astype(BF16)


HALF = 32


def pair_rows(which):
    mine = lax.axis_index("grp") // 2
    return pl.multiple_of((mine if which else 1 - mine) * HALF, HALF)


def exposure_kernel(
    halves, offsets_ref, counts_ref, s0, s1, s4, s3, s2, record_ref, taps_ref, send_ref, *refs
):
    outs, (ext_ref, acc_ref) = refs[:-2], refs[-2:]
    slots, _, width = record_ref.shape
    rows = HALF * len(halves)
    tops = [pl.ds(pair_rows(which), HALF) for which in halves]
    cols = s0.shape[1]
    tap_count = taps_ref.shape[1]
    pieces = width // tap_count
    tiles = width // LANES
    per = tap_count // LANES
    for d, part in enumerate((s0, s1, s2, s3, s4)):
        for h, top in enumerate(tops):
            ext_ref[h * HALF : (h + 1) * HALF, d * cols : (d + 1) * cols] = part[top, :]
    acc_ref[...] = jnp.zeros_like(acc_ref)

    def add_slot(n):
        offset = offsets_ref[n]
        rest = offset % LANES
        base = pl.multiple_of(offset - rest, LANES)
        lane = lane_index((rows, LANES))

        taps = taps_ref[n : n + 1, :]
        wide = jnp.concatenate([taps, jnp.zeros_like(taps)], axis=1)
        band = pltpu.roll(jnp.broadcast_to(wide, (tap_count, 2 * tap_count)), 0, 1, stride=1, stride_axis=0)
        first, second = split(band[:, :tap_count]), split(band[:, tap_count:])

        def banded(x, turn, axis):
            high, low = split(x)
            part_high, part_low = [jnp.concatenate(pair, axis=1 - axis) for pair in zip(first, second)]
            both = lax.dot_general(
                jnp.concatenate([high, low, high], axis=1),
                jnp.concatenate([part_high, part_high, part_low], axis=axis),
                (((1,), (axis,)), ((), ())),
                preferred_element_type=F32,
            )
            k = turn * rows % x.shape[0]
            return both[:, :tap_count] + jnp.concatenate([both[k:, tap_count:], both[:k, tap_count:]], axis=0)

        turned = [
            pltpu.roll(ext_ref[:, pl.ds(base + m * LANES, LANES)], LANES - rest, 1) for m in range(tiles + 1)
        ]
        keep = lane < LANES - rest
        window = [jnp.where(keep, turned[m], turned[m + 1]) for m in range(tiles)]
        stacked = jnp.concatenate(
            [jnp.concatenate(window[p * per : (p + 1) * per], axis=1) for p in range(pieces)], axis=0
        )
        record = jnp.concatenate(
            [record_ref[n, top, p * tap_count : (p + 1) * tap_count] for p in range(pieces) for top in tops], axis=0
        )
        live = jnp.where(counts_ref[:1, :1] > n, 1.0, 0.0)
        residual = (record - banded(stacked, pieces - 1, 0)) * live
        back = banded(residual, 1, 1)
        moved = []
        for m in range(tiles):
            p, h = divmod(m, per)
            moved.append(pltpu.roll(back[p * rows : (p + 1) * rows, h * LANES : (h + 1) * LANES], rest, 1))
        nothing = jnp.zeros((rows, LANES), F32)
        spill = lane < rest
        for m in range(tiles + 1):
            inside = moved[m] if m < tiles else nothing
            earlier = moved[m - 1] if m > 0 else nothing
            acc_ref[:, pl.ds(base + m * LANES, LANES)] += jnp.where(spill, earlier, inside)

    for n in range(slots):
        add_slot(n)

    for h, which in enumerate(halves):
        band = slice(h * HALF, (h + 1) * HALF)
        keep_ref, give_ref = outs[2 * h : 2 * h + 2]
        for d in range(5):
            to_ref = give_ref if d % 2 else keep_ref
            to_ref[:, d // 2 * cols : (d // 2 + 1) * cols] = acc_ref[band, d * cols : (d + 1) * cols]
        if not which:
            give_ref[:, 2 * cols :] = send_ref[...]


def exposure_terms(halves, offsets, counts, sky_parts, exposures, psf_taps, send):
    cols = sky_parts[0].shape[1]
    reach = len(sky_parts) * cols
    shapes = []
    for which in halves:
        shapes += [(HALF, 3 * cols), (HALF, 2 * cols + (0 if which else LANES))]
    near = pl.BlockSpec(memory_space=pltpu.VMEM)
    few = pl.BlockSpec(memory_space=pltpu.SMEM)
    return pl.pallas_call(
        functools.partial(exposure_kernel, halves),
        in_specs=[few] + [near] * (len(sky_parts) + 4),
        out_specs=[near] * len(shapes),
        out_shape=[jax.ShapeDtypeStruct(shape, F32) for shape in shapes],
        scratch_shapes=[pltpu.VMEM((HALF * len(halves), reach), F32)] * 2,
        compiler_params=pltpu.CompilerParams(vmem_limit_bytes=32 << 20),
        cost_estimate=pl.CostEstimate(flops=3_000_000_000 * len(halves), bytes_accessed=2_000_000, transcendentals=0),
    )(offsets, counts, sky_parts[0], sky_parts[1], sky_parts[4], sky_parts[3], sky_parts[2], exposures, psf_taps, send)


def join_kernel(which, keep_ref, got_ref, beside_ref, cross_ref, prior_ref, own_ref, bias_ref, ow_ref, out0, out1, full_ref):
    second = lax.axis_index("sky") % 2 == 1
    low_half = lax.axis_index("grp") % 2
    share, width = out0.shape
    cols = width // 3
    rows = full_ref.shape[0]
    channels = own_ref.shape[0]
    lane = lane_index((channels, LANES))
    beside = beside_ref[:, 2 * cols :]
    from_beside = jnp.logical_xor((lane & 1) == 0, second)
    edge = own_ref[...] + jnp.where(from_beside, beside, cross_ref[...]) + column(bias_ref[...])
    score = jnp.sum(weighted_silu(edge, column(ow_ref[...]) * 0.5), axis=0, keepdims=True)
    lane = lane_index((rows, LANES))
    mine = jnp.where((lane >> 1) == lax.broadcasted_iota(jnp.int32, (rows, LANES), 0), score, 0.0)
    last = jnp.sum(jnp.where((lane & 1) == 0, mine, 0.0), axis=1, keepdims=True)
    first = jnp.sum(jnp.where((lane & 1) == 1, mine, 0.0), axis=1, keepdims=True)
    col = lane_index((rows, cols))
    skipped = prior_ref.shape[0] - rows - 1
    full_ref[...] = (
        prior_ref[skipped : skipped + rows, :]
        + jnp.where(col == 0, first, 0.0)
        + jnp.where(col == cols - 1, last, 0.0)
    )
    for k, out in enumerate((out0, out1)):
        start = pl.multiple_of((low_half ^ k) * share, share)
        top = pl.ds(start, share)
        low = got_ref[top, :cols]
        high = got_ref[top, cols : 2 * cols]
        prior = full_ref[pl.ds(pl.multiple_of(pair_rows(which) + start, share), share), :]
        out[:, :cols] = keep_ref[top, :cols] + prior + jnp.where(second, low, 0.0)
        out[:, cols : 2 * cols] = keep_ref[top, cols : 2 * cols] + jnp.where(second, high, low)
        out[:, 2 * cols :] = keep_ref[top, 2 * cols :] + jnp.where(second, 0.0, high)


def sum_kernel(a, b, c, d, *outs):
    cols = outs[0].shape[1]
    for k, out in enumerate(outs):
        cut = slice(k * cols, (k + 1) * cols)
        out[...] = (a[:, cut] + b[:, cut]) + (c[:, cut] + d[:, cut])


def small_call(kernel, out_shapes, *operands, scratch=()):
    near = pl.BlockSpec(memory_space=pltpu.VMEM)
    return pl.pallas_call(
        kernel,
        in_specs=[near] * len(operands),
        out_specs=[near] * len(out_shapes),
        out_shape=[jax.ShapeDtypeStruct(shape, F32) for shape in out_shapes],
        scratch_shapes=[pltpu.VMEM(shape, F32) for shape in scratch],
        compiler_params=pltpu.CompilerParams(vmem_limit_bytes=8 << 20),
        cost_estimate=pl.CostEstimate(flops=200_000, bytes_accessed=1_000_000, transcendentals=0),
    )(*operands)


def on_device(
    sky_strip, exposures, psf_taps, offsets, counts, features, conv_weight, conv_bias, out_weight
):
    n_grp = lax.axis_size("grp")
    strip_rows, cols = sky_strip.shape
    share = strip_rows // n_grp
    reach_blocks = exposures.shape[2] // cols
    parts = [sky_strip]
    for distance in range(1, reach_blocks + 1):
        parts.append(shifted(sky_strip, "sky", -distance))
    prior, own_edge, send, live = conv_prior(counts, features, conv_weight, conv_bias, out_weight)
    n_sky = lax.axis_size("sky")
    cross = lax.ppermute(send, "sky", [(i, (i - 1 if i % 2 == 0 else i + 1) % n_sky) for i in range(n_sky)])
    keep_a, give_a = exposure_terms((0,), offsets, live, parts, exposures, psf_taps, send)
    keep_b, give_b = exposure_terms((1,), offsets, live, parts, exposures, psf_taps, send)
    got_a = partner(give_a, "sky", 1)
    edges = (cross, prior, own_edge, conv_bias.reshape(1, -1), out_weight.reshape(1, -1))

    def join(which, keep, got):
        return small_call(
            functools.partial(join_kernel, which), [(share, 3 * cols)] * 2, keep, got, got_a, *edges,
            scratch=[(strip_rows, cols)],
        )

    to_2, to_3 = join(0, keep_a, got_a)
    from_2, from_3 = partner(to_2, "grp", 2), partner(to_3, "grp", 3)
    give_b, to_2 = lax.optimization_barrier((give_b, to_2))
    got_b = partner(give_b, "sky", 1)
    kept, to_1 = join(1, keep_b, got_b)
    received = [kept, partner(to_1, "grp", 1), from_2, from_3]
    own, near, distant = small_call(sum_kernel, [(share, cols)] * 3, *received)
    distant = shifted(distant, "sky", 4)
    return own + shifted(near, "sky", 2) + distant


def solution(mesh):
    placed = (
        P(None, "sky"),
        P(("sky", "grp"), None, None),
        P(("sky", "grp"), None),
        P(("sky", "grp")),
        P(("sky", "grp")),
        P(None, None, "sky"),
        P("grp", None, None, None),
        P("grp"),
        P("grp"),
    )
    return jax.shard_map(
        on_device, mesh=mesh, in_specs=placed, out_specs=P("grp", "sky"), check_vma=False
    )
```
